32 devices in a mesh: dp: 16 (over z, y, x), fsdp: 2 (over core).
Axes of the slice: x: 2, y: 2, z: 4, core: 2. Of those that a mesh axis runs over, the one named last changes fastest.
Arguments:
- tokens: bfloat16 [2, 4096, 1024], P(None, ('dp', 'fsdp')), may hold values from -6 to 6
- cotangent: bfloat16 [2, 4096, 1024], P(None, ('dp', 'fsdp')), may hold values from -6 to 6
- lengths: int32 [2, 32], P(None, ('dp', 'fsdp')), may hold values from 32 to 128, as said below
- variate_ids: int32 [2, 4096], P(None, ('dp', 'fsdp')), may hold values from 0 to 3, as said below
- time_ids: int32 [2, 4096], P(None, ('dp', 'fsdp')), may hold values from 0 to 191, as said below
- query_weight: bfloat16 [1024, 1024], P(('dp', 'fsdp')), may hold values from -0.1875 to 0.1875
- key_weight: bfloat16 [1024, 1024], P(('dp', 'fsdp')), may hold values from -0.1875 to 0.1875
- value_weight: bfloat16 [1024, 1024], P(('dp', 'fsdp')), may hold values from -0.1875 to 0.1875
- out_weight: bfloat16 [1024, 1024], P(('dp', 'fsdp')), may hold values from -1 to 1
- gate_weight: bfloat16 [1024, 4096], P(('dp', 'fsdp')), may hold values from -0.1875 to 0.1875
- up_weight: bfloat16 [1024, 4096], P(('dp', 'fsdp')), may hold values from -0.1875 to 0.1875
- down_weight: bfloat16 [4096, 1024], P(('dp', 'fsdp')), may hold values from -0.09375 to 0.09375
- attn_gain: bfloat16 [1024], P(('dp', 'fsdp')), may hold values from 0.5 to 1.5
- ffn_gain: bfloat16 [1024], P(('dp', 'fsdp')), may hold values from 0.5 to 1.5
- variate_bias: float32 [2, 16], replicated, may hold values from -3 to 3
Outputs:
- activations: bfloat16 [2, 4096, 1024], P(None, ('dp', 'fsdp'))
- input_grad: float32 [2, 4096, 1024], P(None, ('dp', 'fsdp'))
- query_weight_grad: float32 [1024, 1024], P(('dp', 'fsdp'))
- key_weight_grad: float32 [1024, 1024], P(('dp', 'fsdp'))
- value_weight_grad: float32 [1024, 1024], P(('dp', 'fsdp'))
- out_weight_grad: float32 [1024, 1024], P(('dp', 'fsdp'))
- gate_weight_grad: float32 [1024, 4096], P(('dp', 'fsdp'))
- up_weight_grad: float32 [1024, 4096], P(('dp', 'fsdp'))
- down_weight_grad: float32 [4096, 1024], P(('dp', 'fsdp'))
- attn_gain_grad: float32 [1024], P(('dp', 'fsdp'))
- ffn_gain_grad: float32 [1024], P(('dp', 'fsdp'))
- variate_bias_grad: float32 [2, 16], replicated
The draws below stay inside these ranges and needn't reach their ends.
Inputs may be any that keep to these rules, and one draw needn't show every extreme that they name: `lengths`: some slot holds exactly 128 real positions and some exactly 32. `variate_ids`: within a slot the variate ids never fall. `time_ids`: within one variate's run of positions the time ids rise by one a position.
All inputs are finite; a program needn't handle non-finite values.
Results may differ from the reference program's by a relative error of at most 0.02.
Values may be sent and summed in bfloat16 or wider, within the bound.
No kernel may reach another device: no remote copies, remote signals or barrier semaphores. Data moves between devices by JAX's collectives and lax.ppermute only.
A program may use at most 256 MiB of HBM per device.

```python
from functools import partial
import jax
import jax.numpy as jnp
from jax import lax

D = 1024
H = 16
FF = 4096
SEQ = 128
MB = 2
SEQS = 32


def draw_lengths(key, part):
    count = MB * SEQS
    drawn = jax.random.randint(key, (count,), SEQ // 4, SEQ + 1)
    chosen = jax.random.randint(jax.random.fold_in(key, 1), (), 0, count)
    drawn = drawn.at[chosen].set(SEQ)
    drawn = drawn.at[(chosen + 1) % count].set(SEQ // 4)
    return drawn.reshape(MB, SEQS).astype(jnp.int32)


def series_layout(key):
    count = MB * SEQS
    cuts = jax.random.randint(jax.random.fold_in(key, 7), (count, 3), 1, SEQ)
    positions = jnp.arange(SEQ, dtype=jnp.int32)
    passed = positions[None, None, :] >= cuts[:, :, None]
    variates = jnp.sum(passed.astype(jnp.int32), axis=1)
    starts = jnp.max(jnp.where(passed, cuts[:, :, None], 0), axis=1)
    offsets = jax.random.randint(jax.random.fold_in(key, 8), (count, 4), 0, 64)
    offsets = offsets.at[0, 0].set(0)
    offsets = offsets.at[count - 1, 3].set(64 + jnp.max(cuts[count - 1]))
    shifted = jnp.take_along_axis(offsets, variates, axis=1)
    stamps = positions[None, :] - starts + shifted
    return (variates.reshape(MB, SEQS * SEQ).astype(jnp.int32), stamps.reshape(MB, SEQS * SEQ).astype(jnp.int32))


def draw_variate_ids(key, part):
    return series_layout(key)[0]


def draw_time_ids(key, part):
    return series_layout(key)[1]


def block_levels(rng, dims, shards, smallest, largest):
    def one(axis_at, blocks):
        heights = jax.random.uniform(jax.random.fold_in(jax.random.fold_in(rng, 6), axis_at), (blocks,), jnp.float32, smallest / len(shards), largest / len(shards))
        return jnp.repeat(jnp.exp(heights), dims[axis_at] // blocks).reshape((-1,) + (1,) * (len(dims) - axis_at - 1))

    factor_of = one(*shards[0])
    for cut in shards[1:]:
        factor_of = factor_of * one(*cut)
    return factor_of


def normal_values(rng, shape, scale, reach, split=(), kind=jnp.bfloat16):
    level = block_levels(rng, shape, split, -0.22, 0.18) if split else 1.0
    array = jax.random.normal(rng, shape, jnp.float32) * scale * level
    return jnp.minimum(jnp.maximum(array, -reach), reach).astype(kind)


def setup_inputs(seed: int = 0) -> dict:
    streams_of = jax.random.split(jax.random.key(seed), 16)
    return {
        "tokens": normal_values(streams_of[0], (MB, SEQS * SEQ, D), 1.0, 6.0, ((1, 32),)),
        "cotangent": normal_values(streams_of[1], (MB, SEQS * SEQ, D), 1.0, 6.0, ((1, 32),)),
        "lengths": draw_lengths(jax.random.fold_in(streams_of[15], 71), 0),
        "variate_ids": draw_variate_ids(jax.random.fold_in(streams_of[15], 71), 0),
        "time_ids": draw_time_ids(jax.random.fold_in(streams_of[15], 71), 0),
        "query_weight": normal_values(streams_of[5], (D, D), D ** -0.5, 0.1875, ((0, 32),)),
        "key_weight": normal_values(streams_of[6], (D, D), D ** -0.5, 0.1875, ((0, 32),)),
        "value_weight": normal_values(streams_of[7], (D, D), D ** -0.5, 0.1875, ((0, 32),)),
        "out_weight": normal_values(streams_of[8], (D, D), (D * 4 // SEQ) ** -0.5, 1.0, ((0, 32),)),
        "gate_weight": normal_values(streams_of[9], (D, FF), D ** -0.5, 0.1875, ((0, 32),)),
        "up_weight": normal_values(streams_of[10], (D, FF), D ** -0.5, 0.1875, ((0, 32),)),
        "down_weight": normal_values(streams_of[11], (FF, D), FF ** -0.5, 0.09375, ((0, 32),)),
        "attn_gain": jnp.clip(1.0 + 0.1 * jax.random.normal(streams_of[12], (D,), jnp.float32), 0.5, 1.5).astype(jnp.bfloat16),
        "ffn_gain": jnp.clip(1.0 + 0.1 * jax.random.normal(streams_of[13], (D,), jnp.float32), 0.5, 1.5).astype(jnp.bfloat16),
        "variate_bias": normal_values(streams_of[14], (2, H), 1.0, 3.0, (), jnp.float32),
    }


EPSILON = 1e-05
SCORE_SCALE = 0.125
NEGATIVE = -1e+30

@jax.custom_vjp
def low(v):
    return lax.optimization_barrier(v.astype(jnp.bfloat16)).astype(jnp.float32)

@jax.custom_vjp
def low_back(v):
    return v

def low_keep(v):
    return (low(v), None)

def low_pass(kept, grad):
    return (grad,)

def back_keep(v):
    return (v, None)

def back_low(kept, grad):
    return (low(grad),)
low.defvjp(low_keep, low_pass)
low_back.defvjp(back_keep, back_low)

def rms_norm(values, gain):
    return values * lax.rsqrt(lax.optimization_barrier(jnp.mean(values * values, axis=-1, keepdims=True)) + EPSILON) * gain

def rotate(values, cosine, sine):
    half = values.shape[-1] // 2
    first = values[..., :half]
    second = values[..., half:]
    return jnp.concatenate([first * cosine - second * sine, second * cosine + first * sine], axis=-1)

def layer(params, inputs, length, variate, times):
    wq, wk, wv, wo, wg, wu, wd, gain_one, gain_two, bias = params
    batch, seq_len, width = inputs.shape
    heads = bias.shape[1]
    head_size = width // heads
    half = head_size // 2
    product = partial(jnp.einsum, precision=lax.Precision.HIGHEST)
    inverse = 10000.0 ** (-jnp.arange(half, dtype=jnp.float32) / half)
    angles = times.astype(jnp.float32)[:, :, None] * inverse[None, None, :]
    cosine = jnp.cos(angles)[:, :, None, :]
    sine = jnp.sin(angles)[:, :, None, :]
    first_normalized = low(rms_norm(inputs, gain_one))
    queries = low(rotate(low_back(product('bld,de->ble', first_normalized, wq)).reshape(batch, seq_len, heads, head_size), cosine, sine))
    keys = low(rotate(low_back(product('bld,de->ble', first_normalized, wk)).reshape(batch, seq_len, heads, head_size), cosine, sine))
    values = low(low_back(product('bld,de->ble', first_normalized, wv))).reshape(batch, seq_len, heads, head_size)
    raw = product('bqhe,bkhe->bhqk', queries, keys) * SCORE_SCALE
    same = variate[:, :, None] == variate[:, None, :]
    raw = raw + jnp.where(same[:, None], bias[0][None, :, None, None], bias[1][None, :, None, None])
    raw = low_back(raw)
    valid = jnp.arange(seq_len, dtype=jnp.int32)[None, None, None, :] < length[:, None, None, None]
    raw = jnp.where(valid, raw, NEGATIVE)
    probs = jax.nn.softmax(raw, axis=-1)
    attended = low(low_back(product('bhqk,bkhe->bqhe', low(probs), values).reshape(batch, seq_len, width)))
    hidden = inputs + low_back(product('bld,de->ble', attended, wo))
    second_normalized = low(rms_norm(hidden, gain_two))
    gate = low_back(product('bld,df->blf', second_normalized, wg))
    upward = low_back(product('bld,df->blf', second_normalized, wu))
    activated = low(jax.nn.silu(gate) * upward)
    return hidden + low_back(product('blf,fd->bld', activated, wd))

def reference(tokens, cotangent, lengths, variate_ids, time_ids, query_weight, key_weight, value_weight, out_weight, gate_weight, up_weight, down_weight, attn_gain, ffn_gain, variate_bias):
    params = (query_weight.astype(jnp.float32), key_weight.astype(jnp.float32), value_weight.astype(jnp.float32), out_weight.astype(jnp.float32), gate_weight.astype(jnp.float32), up_weight.astype(jnp.float32), down_weight.astype(jnp.float32), attn_gain.astype(jnp.float32), ffn_gain.astype(jnp.float32), variate_bias.astype(jnp.float32))
    inputs = tokens.astype(jnp.float32).reshape(MB, SEQS, SEQ, D).transpose(1, 0, 2, 3)
    upstream = cotangent.astype(jnp.float32).reshape(MB, SEQS, SEQ, D).transpose(1, 0, 2, 3)
    slot_lengths = lengths.T
    variates = variate_ids.reshape(MB, SEQS, SEQ).transpose(1, 0, 2)
    stamps = time_ids.reshape(MB, SEQS, SEQ).transpose(1, 0, 2)

    def forward(params, inputs):

        def one_slot(saved_entry):
            return jax.checkpoint(layer)(params, saved_entry[0], saved_entry[1], saved_entry[2], saved_entry[3])
        return lax.map(one_slot, (inputs, slot_lengths, variates, stamps))
    output, pullback = jax.vjp(forward, params, inputs)
    grads, input_grad = pullback(upstream)
    activations = output.transpose(1, 0, 2, 3).reshape(MB, SEQS * SEQ, D).astype(jnp.bfloat16)
    input_grad = input_grad.transpose(1, 0, 2, 3).reshape(MB, SEQS * SEQ, D)
    return (activations, input_grad, grads[0], grads[1], grads[2], grads[3], grads[4], grads[5], grads[6], grads[7], grads[8], grads[9])
```

```python
import jax
import jax.numpy as jnp
from jax import lax
from jax.sharding import PartitionSpec as P

EPSILON = 1e-05
SCORE_SCALE = 0.125
NEGATIVE = -1e30
AXES = ("dp", "fsdp")
UNITS = 4

F32 = jnp.float32
BF16 = jnp.bfloat16


def dot(left, right, contract):
    return lax.dot_general(left, right, ((contract[:1], contract[1:]), ((), ())), preferred_element_type=F32)


class Links:
    def __init__(self, mesh):
        self.count = mesh.shape["dp"] * mesh.shape["fsdp"]
        self.bits = self.count.bit_length() - 1
        self.index = lax.axis_index("dp") * mesh.shape["fsdp"] + lax.axis_index("fsdp")

    def swap(self, value, mask):
        return lax.ppermute(value, AXES, [(i, i ^ mask) for i in range(self.count)])

    def bit(self, position):
        return (self.index >> position) & 1

    def gather(self, piece, positions):
        full = piece[None]
        for position in positions:
            other = self.swap(full, 1 << position)
            high = self.bit(position) == 1
            full = jnp.stack([jnp.where(high, other, full), jnp.where(high, full, other)], axis=1)
            full = full.reshape((-1,) + piece.shape)
        return full.reshape((-1,) + piece.shape[1:])

    def scatter(self, full, positions):
        blocks = full.reshape((2 ** len(positions), -1) + full.shape[1:])
        for position in positions:
            blocks = blocks.reshape((-1, 2) + blocks.shape[1:])
            mine = self.bit(position)
            away = lax.dynamic_index_in_dim(blocks, 1 - mine, 1, keepdims=False).astype(BF16)
            own = lax.dynamic_index_in_dim(blocks, mine, 1, keepdims=False).astype(F32)
            blocks = own + self.swap(away, 1 << position).astype(F32)
        return blocks[0]

    def unit_gather(self, rows):
        pair = jnp.concatenate([rows, self.swap(rows, 2)], axis=0)
        return jnp.concatenate([pair, self.swap(pair, 1)], axis=0)

    def unit_scatter(self, partial):
        half = partial.shape[0] // 2
        pair = partial[:half] + self.swap(partial[half:].astype(BF16), 1).astype(F32)
        half = half // 2
        return pair[:half] + self.swap(pair[half:].astype(BF16), 2).astype(F32)

    def unit_exchange(self, chunks):
        far = self.swap(jnp.stack([chunks[2], chunks[3]]), 2)
        near = self.swap(jnp.stack([chunks[1], far[1]]), 1)
        return [chunks[0], near[0], far[0], near[1]]

    def natural(self, relative):
        low, high = self.bit(0) == 1, self.bit(1) == 1
        a, b, c, d = relative
        a, b, c, d = jnp.where(low, b, a), jnp.where(low, a, b), jnp.where(low, d, c), jnp.where(low, c, d)
        return jnp.where(high, c, a), jnp.where(high, d, b), jnp.where(high, a, c), jnp.where(high, b, d)

    def for_unit(self, blocks, j, axis):
        unit = (self.index % UNITS) ^ j
        return lax.dynamic_index_in_dim(blocks, unit, axis, keepdims=False)


def inverse_norm(values):
    return lax.rsqrt(jnp.mean(values * values, axis=-1, keepdims=True) + EPSILON)


def norm_back(values, scale_inv, weighted):
    inner = jnp.mean(values * weighted, axis=-1, keepdims=True)
    return scale_inv * weighted - values * (scale_inv * scale_inv * scale_inv) * inner


def rotate(values, cosine, sine):
    half = values.shape[-1] // 2
    first = values[..., :half]
    second = values[..., half:]
    return jnp.concatenate([first * cosine - second * sine, second * cosine + first * sine], axis=-1)


def attention_parts(queries, keys, bias, valid, same):
    raw = jnp.einsum("sqhe,skhe->shqk", queries, keys, preferred_element_type=F32) * SCORE_SCALE
    raw = raw + jnp.where(same[:, None], bias[0][None, :, None, None], bias[1][None, :, None, None])
    return jnp.where(valid[:, None, None, :], raw, NEGATIVE)


def solution(mesh):
    def shards(
        tokens,
        cotangent,
        lengths,
        variate_ids,
        time_ids,
        query_weight,
        key_weight,
        value_weight,
        out_weight,
        gate_weight,
        up_weight,
        down_weight,
        attn_gain,
        ffn_gain,
        variate_bias,
    ):
        links = Links(mesh)
        micros, seq, width = tokens.shape
        rows = micros * seq
        heads = variate_bias.shape[1]
        head_size = width // heads
        own_rows = query_weight.shape[0]
        ranks = links.count // UNITS
        hidden_units = gate_weight.shape[1]
        unit_heads = heads // UNITS
        unit_width = width // UNITS
        unit_hidden = hidden_units // UNITS
        down_position = list(range(links.bits - 1, 1, -1))
        up_position = down_position[::-1]
        all_down = list(range(links.bits - 1, -1, -1))
        all_up = all_down[::-1]

        gain_one = attn_gain.astype(F32)[:, None]
        gain_two = ffn_gain.astype(F32)[:, None]
        own_tokens = tokens.reshape(rows, width)
        own_cotangent = cotangent.reshape(rows, width)

        ids = jnp.concatenate(
            [variate_ids.reshape(-1), time_ids.reshape(-1), jnp.broadcast_to(lengths, (micros, seq)).reshape(-1)]
        ).astype(BF16)
        meta_rows = -(-ids.shape[0] // width)
        meta_rows = -(-meta_rows // 16) * 16
        meta = jnp.zeros((meta_rows * width,), BF16).at[: ids.shape[0]].set(ids).reshape(meta_rows, width)
        spread = links.unit_gather(jnp.concatenate([own_tokens, meta], axis=0)).reshape(UNITS, rows + meta_rows, width)
        all_tokens = spread[:, :rows].reshape(UNITS * rows, width)
        ids_all = spread[:, rows:].reshape(UNITS, -1)[:, : 3 * rows].astype(jnp.int32).reshape(UNITS, 3, micros, seq)
        variates = ids_all[:, 0].reshape(UNITS * micros, seq)
        times = ids_all[:, 1].reshape(UNITS * micros, seq)
        sizes = ids_all[:, 2].reshape(UNITS * micros, seq)[:, :1]

        def scaled(weight, gain):
            return (weight.astype(F32) * gain).astype(BF16)

        qkv_blocks = jnp.stack(
            [scaled(w, gain_one).reshape(own_rows, UNITS, unit_width) for w in (query_weight, key_weight, value_weight)],
            axis=1,
        )
        qkv_chunks = [links.for_unit(qkv_blocks, j, 2).reshape(own_rows, 3 * unit_width) for j in range(UNITS)]
        qkv_piece = jnp.concatenate(links.natural(links.unit_exchange(qkv_chunks)), axis=0)
        wqkv = links.gather(qkv_piece, down_position)
        wo = links.gather(out_weight, all_down)
        gu_blocks = jnp.stack(
            [
                scaled(w, gain_two).reshape(own_rows, ranks, UNITS, unit_hidden // ranks)
                for w in (gate_weight, up_weight)
            ],
            axis=1,
        )
        gu_chunks = [links.for_unit(gu_blocks, j, 3).reshape(own_rows, 2 * unit_hidden) for j in range(UNITS)]
        gu_piece = jnp.concatenate(links.natural(links.unit_exchange(gu_chunks)), axis=0)
        wgu = links.gather(gu_piece, down_position)
        wd = links.gather(down_weight, down_position)
        all_cotangent = links.unit_gather(own_cotangent)

        token_values = all_tokens.astype(F32)
        normed = (token_values * inverse_norm(token_values)).astype(BF16)
        projected = dot(normed, wqkv, (1, 0)).reshape(UNITS * micros, seq, 3, unit_heads, head_size)
        half = head_size // 2
        inverse = 10000.0 ** (-jnp.arange(half, dtype=F32) / half)
        angles = times.astype(F32)[:, :, None] * inverse
        cosine = jnp.cos(angles)[:, :, None, :]
        sine = jnp.sin(angles)[:, :, None, :]
        queries = rotate(projected[:, :, 0], cosine, sine).astype(BF16)
        keys = rotate(projected[:, :, 1], cosine, sine).astype(BF16)
        values = projected[:, :, 2].astype(BF16)
        bias = lax.dynamic_slice_in_dim(variate_bias, (links.index % UNITS) * unit_heads, unit_heads, 1)
        valid = jnp.arange(seq, dtype=jnp.int32)[None, :] < sizes
        same = variates[:, :, None] == variates[:, None, :]
        scores = attention_parts(queries, keys, bias, valid, same)
        peak = jnp.max(scores, axis=-1, keepdims=True)
        log_total = peak + jnp.log(jnp.sum(jnp.exp(scores - peak), axis=-1, keepdims=True))
        probs = jnp.exp(scores - log_total)
        attended = jnp.einsum("shqk,skhe->sqhe", probs.astype(BF16), values, preferred_element_type=F32)
        attended = attended.astype(BF16).reshape(UNITS, rows, unit_width)
        order = (0, 2, 1, 3)
        back = [order.index(j) for j in range(UNITS)]
        heads_of = links.unit_exchange([attended[back[j]] for j in range(UNITS)])
        own_attended = jnp.concatenate(links.natural(heads_of), axis=1)
        inputs = own_tokens.astype(F32)
        hidden = inputs + dot(own_attended, wo, (1, 0))

        inv_two = inverse_norm(hidden)
        normed_two = links.unit_gather((hidden * inv_two).astype(BF16))
        both = dot(normed_two, wgu, (1, 0))
        gate, upward = both[:, :unit_hidden], both[:, unit_hidden:]
        sigmoid = jax.nn.sigmoid(gate)
        activated = (gate * sigmoid * upward).astype(BF16)
        output = (hidden + links.unit_scatter(dot(activated, wd, (1, 0)))).astype(BF16)
        activated_grad = dot(all_cotangent, wd, (1, 1))
        gate_grad = (activated_grad * upward * sigmoid * (1.0 + gate * (1.0 - sigmoid))).astype(BF16)
        up_grad = (activated_grad * gate * sigmoid).astype(BF16)
        both_grad = jnp.concatenate([gate_grad, up_grad], axis=1)
        weighted_two = links.unit_scatter(dot(both_grad, wgu, (1, 1)))
        d_down = dot(activated, all_cotangent, (0, 0)).astype(BF16)
        d_both = dot(normed_two, both_grad, (0, 0)).astype(BF16)
        hidden_grad = own_cotangent.astype(F32) + norm_back(hidden, inv_two, weighted_two)
        hidden_low = hidden_grad.astype(BF16)

        own_attended_grad = dot(hidden_low, wo, (1, 1)).astype(BF16).reshape(rows, UNITS, unit_width)
        rows_of = links.unit_exchange([links.for_unit(own_attended_grad, j, 1) for j in range(UNITS)])
        attended_grad = jnp.concatenate([rows_of[j] for j in order], axis=0)
        attended_grad = attended_grad.reshape(UNITS * micros, seq, unit_heads, head_size)
        d_out = dot(own_attended, hidden_low, (0, 0)).astype(BF16)
        prob_grad = jnp.einsum("sqhe,skhe->shqk", attended_grad, values, preferred_element_type=F32)
        row_inner = jnp.sum(probs * prob_grad, axis=-1, keepdims=True)
        score_grad = (probs * (prob_grad - row_inner)).astype(BF16)
        wide = score_grad.astype(F32)
        same_sum = jnp.sum(jnp.where(same[:, None], wide, 0.0), axis=(0, 2, 3))
        other_sum = jnp.sum(jnp.where(same[:, None], 0.0, wide), axis=(0, 2, 3))
        value_low = jnp.einsum("shqk,sqhe->skhe", probs.astype(BF16), attended_grad, preferred_element_type=F32)
        query_grad = jnp.einsum("shqk,skhe->sqhe", score_grad, keys, preferred_element_type=F32) * SCORE_SCALE
        key_grad = jnp.einsum("shqk,sqhe->skhe", score_grad, queries, preferred_element_type=F32) * SCORE_SCALE
        lows = jnp.stack([rotate(query_grad, cosine, -sine), rotate(key_grad, cosine, -sine), value_low], axis=2)
        lows = lows.astype(BF16).reshape(UNITS * rows, 3 * unit_width)
        d_qkv = dot(normed, lows, (0, 0)).astype(BF16)
        weighted_one = links.unit_scatter(dot(lows, wqkv, (1, 1)))
        input_grad = hidden_grad + norm_back(inputs, inverse_norm(inputs), weighted_one)

        own_down = links.scatter(d_down, up_position)

        def columns_back(full):
            piece = links.scatter(full, up_position).astype(BF16).reshape(UNITS, own_rows, -1)
            got = links.unit_exchange([links.for_unit(piece, j, 0) for j in range(UNITS)])
            return links.natural(got)

        gu_parts = jnp.stack(columns_back(d_both)).astype(F32)
        gu_parts = gu_parts.reshape(UNITS, own_rows, 2, ranks, unit_hidden // ranks).transpose(2, 1, 3, 0, 4)
        gu_own = gu_parts.reshape(2, own_rows, hidden_units)
        own_out = links.scatter(d_out, all_up)
        qkv_parts = jnp.stack(columns_back(d_qkv)).astype(F32)
        qkv_parts = qkv_parts.reshape(UNITS, own_rows, 3, unit_width).transpose(2, 1, 0, 3)
        qkv_own = qkv_parts.reshape(3, own_rows, width)
        attn_gain_grad = sum(
            jnp.sum(w.astype(F32) * g, axis=1) for w, g in zip((query_weight, key_weight, value_weight), qkv_own)
        )
        ffn_gain_grad = sum(jnp.sum(w.astype(F32) * g, axis=1) for w, g in zip((gate_weight, up_weight), gu_own))

        sums = jnp.stack([same_sum, other_sum])
        sums = lax.dynamic_update_slice(
            jnp.zeros((2, heads), F32), sums, (0, (links.index % UNITS) * unit_heads)
        )
        for position in range(links.bits):
            sums = sums + links.swap(sums, 1 << position)

        return (
            output.reshape(tokens.shape),
            input_grad.reshape(tokens.shape),
            qkv_own[0] * gain_one,
            qkv_own[1] * gain_one,
            qkv_own[2] * gain_one,
            own_out,
            gu_own[0] * gain_two,
            gu_own[1] * gain_two,
            own_down,
            attn_gain_grad,
            ffn_gain_grad,
            sums,
        )

    along = P(None, AXES, None)
    line = P(None, AXES)
    block = P(AXES, None)
    return jax.shard_map(
        shards,
        mesh=mesh,
        in_specs=(along, along, line, line, line) + (block,) * 7 + (P(AXES), P(AXES), P()),
        out_specs=(along, along) + (block,) * 7 + (P(AXES), P(AXES), P()),
        check_vma=False,
    )
```
